32 devices in a mesh: tm: 8 (over z, x), clip: 4 (over y, core).
Axes of the slice: x: 2, y: 2, z: 4, core: 2. Of those that a mesh axis runs over, the one named last changes fastest.
Arguments:
- video: float32 [4, 8, 16, 32, 320], P('clip', 'tm'), may hold values from -6 to 6
- spatial_w: bfloat16 [9, 320, 320], P(None, 'clip'), may hold values from -0.109375 to 0.109375
- spatial_b: float32 [320], replicated, may hold values from -3 to 3
- temporal_w: float32 [3, 320, 320], P(None, 'clip'), may hold values from -0.1875 to 0.1875
- cotangent: float32 [4, 8, 16, 32, 320], P('clip', 'tm'), may hold values from -6 to 6
Outputs:
- output: float32 [4, 8, 16, 32, 320], P('clip', 'tm')
- grad_video: float32 [4, 8, 16, 32, 320], P('clip', 'tm')
- grad_temporal: float32 [3, 320, 320], P(None, 'clip')
The draws below stay inside these ranges and needn't reach their ends.
All inputs are finite; a program needn't handle non-finite values.
Results may differ from the reference program's by a relative error of at most 0.0049.
Values may be sent and summed in bfloat16 or wider, within the bound.
A program may use at most 64 MiB of HBM per device.

```python
import math
import jax
import jax.numpy as jnp
from jax import lax

C = 320
HEIGHT = 16
WIDTH = 32
FRAMES = 8
CLIPS = 4
ROWS_ALL = 16384


def steps_of(rng, extent, split, low, high):
    gain, own = 1.0, jax.random.fold_in(rng, 6)
    for axis_at, blocks in split:
        draws = jnp.exp(jax.random.uniform(jax.random.fold_in(own, axis_at), (blocks,), jnp.float32, low / len(split), high / len(split)))
        gain = gain * jnp.repeat(draws, extent[axis_at] // blocks).reshape([-1 if axis == axis_at else 1 for axis in range(len(extent))])
    return gain


def bell_draw(key, extent, deviation, bound, shards=(), kind=jnp.bfloat16):
    values = deviation * jax.random.normal(key, extent, jnp.float32)
    if shards:
        values = values * steps_of(key, extent, shards, -0.22, 0.18)
    return jnp.clip(values, -bound, bound).astype(kind)


def setup_inputs(seed: int = 0) -> dict:
    splits = jax.random.split(jax.random.key(seed), 6)
    video = bell_draw(splits[0], (CLIPS, FRAMES, HEIGHT, WIDTH, C), 1.0, 6.0, ((0, 4), (1, 8)), jnp.float32)
    spatial_w = bell_draw(splits[1], (9, C, C), (9 * C) ** -0.5, 0.109375, ((1, 4),))
    spatial_b = bell_draw(splits[2], (C,), 0.5, 3.0, (), jnp.float32)
    temporal_w = bell_draw(splits[3], (3, C, C), (3 * C) ** -0.5, 0.1875, ((1, 4),), jnp.float32)
    cotangent = bell_draw(splits[4], (CLIPS, FRAMES, HEIGHT, WIDTH, C), 1.0, 6.0, ((0, 4), (1, 8)), jnp.float32)
    return {"video": video, "spatial_w": spatial_w, "spatial_b": spatial_b, "temporal_w": temporal_w, "cotangent": cotangent}


def outer_dot(left, right):
    return lax.dot_general(left, right, (((0,), (0,)), ((), ())), preferred_element_type=jnp.float32)

def transpose_dot(left, right):
    return lax.dot_general(left, right, (((1,), (1,)), ((), ())), preferred_element_type=jnp.float32)

def one_clip(video, cotangent, spatial_w, spatial_b, temporal_b):
    frames, height, width, chans = video.shape
    row_count = frames * height * width
    video_b = video.astype(jnp.bfloat16)
    padded = jnp.pad(video_b, ((0, 0), (1, 1), (1, 1), (0, 0)))
    spatial = jnp.zeros((row_count, chans), jnp.float32)
    for shift_y in range(3):
        for shift_x in range(3):
            columns = padded[:, shift_y:shift_y + height, shift_x:shift_x + width, :].reshape(row_count, chans)
            spatial = spatial + jnp.dot(columns, spatial_w[3 * shift_y + shift_x], preferred_element_type=jnp.float32)
    spatial = spatial + spatial_b
    sigmoid_s = jax.nn.sigmoid(spatial)
    hidden = (spatial * sigmoid_s).astype(jnp.bfloat16).reshape(frames, height, width, chans)
    hidden_pad = jnp.pad(hidden, ((1, 1), (0, 0), (0, 0), (0, 0)))
    temporal = jnp.zeros((row_count, chans), jnp.float32)
    for kernel_tap in range(3):
        shifted = hidden_pad[kernel_tap:kernel_tap + frames].reshape(row_count, chans)
        temporal = temporal + jnp.dot(shifted, temporal_b[kernel_tap], preferred_element_type=jnp.float32)
    output = video + temporal.reshape(video.shape)
    cot_b = cotangent.astype(jnp.bfloat16)
    cot_flat = cot_b.reshape(row_count, chans)
    cot_pad = jnp.pad(cot_b, ((1, 1), (0, 0), (0, 0), (0, 0)))
    grad_hidden = jnp.zeros((row_count, chans), jnp.float32)
    grads = []
    for kernel_tap in range(3):
        shifted_cot = cot_pad[2 - kernel_tap:2 - kernel_tap + frames].reshape(row_count, chans)
        grad_hidden = grad_hidden + transpose_dot(shifted_cot, temporal_b[kernel_tap])
        shifted_hid = hidden_pad[kernel_tap:kernel_tap + frames].reshape(row_count, chans)
        grads.append(outer_dot(shifted_hid, cot_flat))
    grad_spatial = (grad_hidden * sigmoid_s * (1.0 + spatial * (1.0 - sigmoid_s))).astype(jnp.bfloat16)
    grad_pad = jnp.zeros((frames, height + 2, width + 2, chans), jnp.float32)
    for shift_y in range(3):
        for shift_x in range(3):
            contrib = transpose_dot(grad_spatial, spatial_w[3 * shift_y + shift_x]).reshape(frames, height, width, chans)
            grad_pad = grad_pad.at[:, shift_y:shift_y + height, shift_x:shift_x + width, :].add(contrib)
    grad_video = cotangent + grad_pad[:, 1:-1, 1:-1, :]
    return (output, grad_video, jnp.stack(grads))

def reference(video, spatial_w, spatial_b, temporal_w, cotangent):
    temporal_b = temporal_w.astype(jnp.bfloat16)

    def per_clip(pair):
        return one_clip(pair[0], pair[1], spatial_w, spatial_b, temporal_b)
    output, grad_video, grads = lax.map(per_clip, (video, cotangent))
    grad_temporal = lax.optimization_barrier(jnp.sum(grads, axis=0)) * (1.0 / math.sqrt(ROWS_ALL))
    return (output, grad_video, grad_temporal)
```

```python
import functools
import math

import jax
import jax.numpy as jnp
from jax import lax
from jax.experimental import pallas as pl
from jax.experimental.pallas import tpu as pltpu
from jax.sharding import PartitionSpec as P

F32 = jnp.float32
BF16 = jnp.bfloat16
MESH = pl.DeviceIdType.MESH


def nn_dot(left, right):
    return lax.dot_general(left, right, (((1,), (0,)), ((), ())), preferred_element_type=F32)


def outer_dot(left, right):
    return lax.dot_general(left, right, (((0,), (0,)), ((), ())), preferred_element_type=F32)


def transpose_dot(left, right):
    return lax.dot_general(left, right, (((1,), (1,)), ((), ())), preferred_element_type=F32)


def block_kernel(
    dims,
    video_h, sw_h, bias_ref, tw_h, cot_h,
    out_h, gv_h, gt_h,
    video, cot, tw, wg, xcat, cb, chalo, hb, hhalo, slope, gpad, out_v, gv_v,
    gtl, rx, ysend, ry, psum, pb, rs, mine, ag, gt_v,
    load_sem, w_send, w_recv, halo_send, halo_recv, g_send, g_recv, a_send, a_recv, out_sem,
):
    n_tm, height, width, chans, scale = dims
    rows = height * width
    depth = sw_h.shape[1]
    half = rows // 2
    tm = lax.axis_index("tm")
    c = lax.axis_index("clip")

    def flip(value, bit):
        return value + bit - 2 * bit * (lax.rem(value // bit, 2))

    core, ypart = flip(c, 1), flip(c, 2)
    xpart, zpart = flip(tm, 1), flip(tm, 2)
    parity = lax.rem(tm, 2)
    h = lax.rem(tm // 2, 2)

    loads = [
        pltpu.make_async_copy(cot_h, cot, load_sem.at[0]),
        pltpu.make_async_copy(tw_h, tw, load_sem.at[1]),
        pltpu.make_async_copy(
            sw_h, wg.at[pl.ds(0, 9), pl.ds(pl.multiple_of(c * depth, 16), depth), :], load_sem.at[2]
        ),
        pltpu.make_async_copy(video_h, video, load_sem.at[3]),
    ]
    for load in loads:
        load.start()

    barrier = pltpu.get_barrier_semaphore()
    for step in range(1, n_tm):
        pl.semaphore_signal(
            barrier, inc=1, device_id=(lax.rem(tm + step, n_tm), c), device_id_type=MESH
        )
    pl.semaphore_signal(barrier, inc=1, device_id=(tm, core), device_id_type=MESH)
    pl.semaphore_signal(barrier, inc=1, device_id=(tm, ypart), device_id_type=MESH)

    def band(owner, first, count=3):
        return wg.at[pl.ds(first, count), pl.ds(pl.multiple_of(owner * depth, 16), depth), :]

    loads[0].wait()
    cb[...] = cot[...].astype(BF16)
    loads[1].wait()
    wg[9:12, pl.ds(pl.multiple_of(c * depth, 16), depth), :] = tw[...].astype(BF16)
    loads[2].wait()
    pl.semaphore_wait(barrier, n_tm + 1)

    def send(src, dst, ssem, rsem, device):
        copy = pltpu.make_async_remote_copy(
            src_ref=src, dst_ref=dst, send_sem=ssem, recv_sem=rsem,
            device_id=device, device_id_type=MESH,
        )
        copy.start()
        return copy

    def wsend(slot, owner, first, device):
        return send(band(owner, first), band(owner, first), w_send.at[slot], w_recv.at[slot], device)

    y_copies = [wsend(j, c, 6 * h + 3 * j, (tm, ypart)) for j in range(2)]

    def hsend(slot, src, dst, device):
        return send(src, dst, halo_send.at[slot], halo_recv.at[slot], device)

    def near_sends(base, own, halo):
        return [
            hsend(
                base + q,
                own.at[pl.ds(q * half, half), :],
                halo.at[parity, pl.ds(q * half, half), :],
                (xpart, c),
            )
            for q in range(2)
        ]

    def far_copy(base, halo, q):
        target = tm + 2 - 4 * parity
        target = jnp.clip(target, 0, n_tm - 1)
        return pltpu.make_async_remote_copy(
            src_ref=halo.at[1 - parity, pl.ds(q * half, half), :],
            dst_ref=halo.at[parity, pl.ds(q * half, half), :],
            send_sem=halo_send.at[base + 2 + q],
            recv_sem=halo_recv.at[base + 2 + q],
            device_id=(target, c),
            device_id_type=MESH,
        )

    sends_far = jnp.logical_or(
        jnp.logical_and(parity == 0, tm + 2 < n_tm), jnp.logical_and(parity == 1, tm >= 2)
    )
    gets_far = jnp.logical_or(
        jnp.logical_and(parity == 0, tm >= 2), jnp.logical_and(parity == 1, tm + 2 < n_tm)
    )

    def far_start(base, halo, q):
        @pl.when(sends_far)
        def _():
            far_copy(base, halo, q).start()

    def far_recv(base, halo, q):
        @pl.when(gets_far)
        def _():
            far_copy(base, halo, q).wait_recv()

    def far_done(base, halo, q):
        @pl.when(sends_far)
        def _():
            far_copy(base, halo, q).wait_send()

    cot_near = near_sends(0, cb, chalo)
    own_copies = [wsend(4 + j, c, 3 * j, (tm, core)) for j in range(4)]

    for edge, slot in ((0, 0), (n_tm - 1, 1)):
        @pl.when(tm == edge)
        def _():
            chalo[slot] = jnp.zeros((rows, chans), BF16)
            hhalo[slot] = jnp.zeros((rows, chans), BF16)

    column = lax.rem(lax.broadcasted_iota(jnp.int32, (rows, chans), 0), width)

    def shifted(value, step):
        if step == 0:
            return value
        rolled = pltpu.roll(value, step % rows, 0)
        return jnp.where(column == (0 if step == 1 else width - 1), 0.0, rolled)

    xcat[0:width] = jnp.zeros((width, 3 * chans), BF16)
    xcat[width + rows :] = jnp.zeros((width, 3 * chans), BF16)
    for b in range(3):
        gpad[b, 0:width] = jnp.zeros((width, chans), BF16)
        gpad[b, width + rows :] = jnp.zeros((width, chans), BF16)
    loads[3].wait()
    frame = video[...]
    xcat[width : width + rows] = jnp.concatenate(
        [shifted(frame, 1).astype(BF16), frame.astype(BF16), shifted(frame, -1).astype(BF16)], axis=1
    )

    relays = []
    z_copies = []
    for j in range(2):
        y_copies[j].wait_recv()
        z_copies.append(wsend(2 + j, ypart, 6 * h + 3 * j, (zpart, c)))
        relays.append(wsend(8 + j, ypart, 6 * h + 3 * j, (tm, core)))
        cot_near[j].wait_recv()
        far_start(0, chalo, j)
    for j in range(2):
        z_copies[j].wait_recv()
        relays.append(wsend(10 + j, ypart, 6 * (1 - h) + 3 * j, (tm, core)))
    for copy in own_copies + relays:
        copy.wait_recv()

    hid_near = []
    for q in range(2):
        acc = bias_ref[...] + jnp.zeros((half, chans), F32)
        for a in range(3):
            acc = acc + nn_dot(
                xcat[a * width + q * half : a * width + (q + 1) * half],
                wg[3 * a : 3 * a + 3].reshape(3 * chans, chans),
            )
        sig = jax.nn.sigmoid(acc)
        hb[q * half : (q + 1) * half] = (acc * sig).astype(BF16)
        slope[q * half : (q + 1) * half] = sig * (1.0 + acc * (1.0 - sig))
        hid_near.append(
            hsend(
                4 + q,
                hb.at[pl.ds(q * half, half), :],
                hhalo.at[parity, pl.ds(q * half, half), :],
                (xpart, c),
            )
        )

    for q in range(2):
        far_recv(0, chalo, q)
    n_own = chans // depth
    pad_rows = psum.shape[0]
    hidden_all = hb[...]
    for k in range(3):
        right = (chalo[1], cb[...], chalo[0])[k]
        product = outer_dot(hidden_all, right)
        for owner in range(n_own):
            gtl[owner, k * depth : (k + 1) * depth] = product[owner * depth : (owner + 1) * depth]
    for owner in range(n_own):
        gtl[owner, 3 * depth :] = jnp.zeros((pad_rows - 3 * depth, chans), F32)
    diag = flip(core, 2)
    core_copies = [
        send(gtl.at[diag], rx.at[1], g_send.at[0], g_recv.at[0], (tm, core)),
        send(gtl.at[core], rx.at[0], g_send.at[1], g_recv.at[1], (tm, core)),
    ]

    grad_h = transpose_dot(chalo[1], wg[9]) + transpose_dot(cb[...], wg[10])
    grad_h = grad_h + transpose_dot(chalo[0], wg[11])
    grad_s = grad_h * slope[...]
    for b in range(3):
        gpad[b, width : width + rows] = shifted(grad_s, b - 1).astype(BF16)

    core_copies[0].wait_recv()
    ysend[...] = (gtl[ypart] + rx[1]).astype(BF16)
    grad_y = send(ysend, ry, g_send.at[2], g_recv.at[2], (tm, ypart))
    core_copies[1].wait_recv()
    psum[...] = gtl[c] + rx[0]

    hid_near[0].wait_recv()
    far_start(4, hhalo, 0)

    def grad_conv(q):
        acc = cot[q * half : (q + 1) * half]
        for a in range(3):
            start = (2 - a) * width + q * half
            for b in range(3):
                acc = acc + transpose_dot(gpad[b, start : start + half], wg[3 * a + b])
        gv_v[q * half : (q + 1) * half] = acc

    grad_conv(0)
    hid_near[1].wait_recv()
    far_start(4, hhalo, 1)

    grad_y.wait_recv()
    psum[...] = psum[...] + ry[...].astype(F32)
    pb[...] = psum[...].astype(BF16)
    piece = pad_rows // n_tm
    scatters = []
    for step in range(1, n_tm):
        to = lax.rem(tm + step, n_tm)
        scatters.append(
            send(
                pb.at[pl.ds(pl.multiple_of(to * piece, piece), piece), :],
                rs.at[step - 1], a_send.at[step - 1], a_recv.at[step - 1], (to, c),
            )
        )
    grad_conv(1)
    gv_out = pltpu.make_async_copy(gv_v, gv_h, out_sem.at[0])
    gv_out.start()

    out_v[...] = video[...] + nn_dot(hb[...], wg[10])

    for copy in scatters:
        copy.wait_recv()
    total = psum[pl.ds(pl.multiple_of(tm * piece, piece), piece), :]
    for step in range(1, n_tm):
        total = total + rs[step - 1].astype(F32)
    spot = pl.ds(pl.multiple_of(tm * piece, piece), piece)
    mine[...] = total.astype(BF16)
    gathers = []
    for step in range(1, n_tm):
        to = lax.rem(tm + step, n_tm)
        slot = n_tm - 2 + step
        gathers.append(
            send(mine, ag.at[spot, :], a_send.at[slot], a_recv.at[slot], (to, c))
        )
    ag[spot, :] = total.astype(BF16)

    for q in range(2):
        far_recv(4, hhalo, q)
    out_v[...] = out_v[...] + nn_dot(hhalo[0], wg[9]) + nn_dot(hhalo[1], wg[11])
    out_out = pltpu.make_async_copy(out_v, out_h, out_sem.at[1])
    out_out.start()

    for copy in gathers:
        copy.wait_recv()
    gt_v[...] = (ag[0 : 3 * depth].astype(F32) * scale).reshape(3, depth, chans)
    gt_out = pltpu.make_async_copy(gt_v, gt_h, out_sem.at[2])
    gt_out.start()

    for copy in (
        y_copies + z_copies + own_copies + relays + cot_near + hid_near
        + core_copies + [grad_y] + scatters + gathers
    ):
        copy.wait_send()
    for q in range(2):
        far_done(0, chalo, q)
        far_done(4, hhalo, q)
    gv_out.wait()
    out_out.wait()
    gt_out.wait()


def fused(n_tm, n_clip, video, spatial_w, spatial_b, temporal_w, cotangent):
    clips, frames, height, width, chans = video.shape
    rows = height * width
    depth = spatial_w.shape[1]
    pad_rows = -(-3 * depth // (16 * n_tm)) * 16 * n_tm
    scale = 1.0 / math.sqrt(rows * n_tm * n_clip)
    piece = pad_rows // n_tm
    any_spec = pl.BlockSpec(memory_space=pl.ANY)
    vm = pltpu.VMEM
    dma = pltpu.SemaphoreType.DMA
    out, gv, gt = pl.pallas_call(
        functools.partial(block_kernel, (n_tm, height, width, chans, scale)),
        out_shape=(
            jax.ShapeDtypeStruct((rows, chans), F32),
            jax.ShapeDtypeStruct((rows, chans), F32),
            jax.ShapeDtypeStruct((3, depth, chans), F32),
        ),
        in_specs=[any_spec, any_spec, pl.BlockSpec(memory_space=vm), any_spec, any_spec],
        out_specs=(any_spec, any_spec, any_spec),
        scratch_shapes=[
            vm((rows, chans), F32),
            vm((rows, chans), F32),
            vm((3, depth, chans), F32),
            vm((12, chans, chans), BF16),
            vm((rows + 2 * width, 3 * chans), BF16),
            vm((rows, chans), BF16),
            vm((2, rows, chans), BF16),
            vm((rows, chans), BF16),
            vm((2, rows, chans), BF16),
            vm((rows, chans), F32),
            vm((3, rows + 2 * width, chans), BF16),
            vm((rows, chans), F32),
            vm((rows, chans), F32),
            vm((n_clip, pad_rows, chans), F32),
            vm((2, pad_rows, chans), F32),
            vm((pad_rows, chans), BF16),
            vm((pad_rows, chans), BF16),
            vm((pad_rows, chans), F32),
            vm((pad_rows, chans), BF16),
            vm((n_tm - 1, piece, chans), BF16),
            vm((piece, chans), BF16),
            vm((pad_rows, chans), BF16),
            vm((3, depth, chans), F32),
            dma((4,)),
            dma((12,)),
            dma((12,)),
            dma((8,)),
            dma((8,)),
            dma((3,)),
            dma((3,)),
            dma((2 * n_tm - 2,)),
            dma((2 * n_tm - 2,)),
            dma((3,)),
        ],
        compiler_params=pltpu.CompilerParams(
            collective_id=0, has_side_effects=True, vmem_limit_bytes=48 * 2**20
        ),
        name="block",
    )(
        video.reshape(rows, chans), spatial_w, spatial_b.reshape(1, chans), temporal_w,
        cotangent.reshape(rows, chans),
    )
    return out.reshape(video.shape), gv.reshape(video.shape), gt


def padded_2(cells, sides, width):
    for axis, dim in sides:
        count = lax.axis_size(axis)
        ends = count - 1
        head = lax.slice_in_dim(cells, 0, width, axis=dim)
        tail = lax.slice_in_dim(cells, cells.shape[dim] - width, cells.shape[dim], axis=dim)
        cells = jnp.concatenate(
            [
                lax.ppermute(tail, axis, [(i, (i + 1) % count) for i in range(ends)]),
                cells,
                lax.ppermute(head, axis, [((i + 1) % count, i) for i in range(ends)]),
            ],
            axis=dim,
        )
    return cells


def native(video, spatial_w, spatial_b, temporal_w, cotangent):
    clips, frames, height, width, chans = video.shape
    row_count = clips * frames * height * width
    pads = ((0, 0), (0, 0), (1, 1), (1, 1), (0, 0))
    padded = jnp.pad(video.astype(BF16), pads)
    temporal_b = temporal_w.astype(BF16)
    spatial_all = lax.all_gather(spatial_w, "clip", axis=1, tiled=True)
    temporal_all = lax.all_gather(temporal_b, "clip", axis=1, tiled=True)
    spatial = jnp.zeros((row_count, chans), F32)
    for y in range(3):
        for x in range(3):
            window = padded[:, :, y : y + height, x : x + width, :].reshape(row_count, chans)
            spatial = spatial + nn_dot(window, spatial_all[3 * y + x])
    spatial = spatial + spatial_b
    sigmoid_s = jax.nn.sigmoid(spatial)
    hidden = (spatial * sigmoid_s).astype(BF16).reshape(video.shape)
    hidden_pad = padded_2(hidden, (("tm", 1),), 1)
    cot_b = cotangent.astype(BF16)
    cot_flat = cot_b.reshape(row_count, chans)
    cot_pad = padded_2(cot_b, (("tm", 1),), 1)
    temporal = jnp.zeros((row_count, chans), F32)
    grad_hidden = jnp.zeros((row_count, chans), F32)
    grads = []
    for k in range(3):
        shifted_hid = hidden_pad[:, k : k + frames].reshape(row_count, chans)
        temporal = temporal + nn_dot(shifted_hid, temporal_all[k])
        shifted_cot = cot_pad[:, 2 - k : 2 - k + frames].reshape(row_count, chans)
        grad_hidden = grad_hidden + transpose_dot(shifted_cot, temporal_all[k])
        grads.append(outer_dot(shifted_hid, cot_flat))
    total_rows = row_count * lax.axis_size("tm") * lax.axis_size("clip")
    summed = lax.psum(jnp.stack(grads), "tm")
    owned = lax.psum_scatter(summed, "clip", scatter_dimension=1, tiled=True)
    grad_spatial = (grad_hidden * sigmoid_s * (1.0 + spatial * (1.0 - sigmoid_s))).astype(BF16)
    grad_frames = jnp.pad(grad_spatial.reshape(video.shape), pads)
    grad_acc = cotangent.reshape(row_count, chans)
    for y in range(3):
        for x in range(3):
            window = grad_frames[:, :, 2 - y : 2 - y + height, 2 - x : 2 - x + width, :]
            window = window.reshape(row_count, chans)
            grad_acc = grad_acc + transpose_dot(window, spatial_all[3 * y + x])
    return (
        video + temporal.reshape(video.shape),
        grad_acc.reshape(video.shape),
        owned * (1.0 / math.sqrt(total_rows)),
    )


def solution(mesh):
    n_tm, n_clip = mesh.shape["tm"], mesh.shape["clip"]

    def on_device(video, spatial_w, spatial_b, temporal_w, cotangent):
        args = (video, spatial_w, spatial_b, temporal_w, cotangent)
        one_frame = video.shape[0] == 1 and video.shape[1] == 1
        if one_frame and spatial_w.shape[1] % 16 == 0 and n_clip == 4 and n_tm % 4 == 0:
            return fused(n_tm, n_clip, *args)
        return native(*args)

    return jax.shard_map(
        on_device,
        mesh=mesh,
        in_specs=(
            P("clip", "tm", None, None, None),
            P(None, "clip", None),
            P(),
            P(None, "clip", None),
            P("clip", "tm", None, None, None),
        ),
        out_specs=(
            P("clip", "tm", None, None, None),
            P("clip", "tm", None, None, None),
            P(None, "clip", None),
        ),
        check_vma=False,
    )
```

```python
import functools
import math

import jax
import jax.numpy as jnp
from jax import lax
from jax.experimental import pallas as pl
from jax.experimental.pallas import tpu as pltpu
from jax.sharding import PartitionSpec as P

F32 = jnp.float32
BF16 = jnp.bfloat16
MESH = pl.DeviceIdType.MESH


def nn_dot(left, right):
    return lax.dot_general(left, right, (((1,), (0,)), ((), ())), preferred_element_type=F32)


def outer_dot(left, right):
    return lax.dot_general(left, right, (((0,), (0,)), ((), ())), preferred_element_type=F32)


def transpose_dot(left, right):
    return lax.dot_general(left, right, (((1,), (1,)), ((), ())), preferred_element_type=F32)


def block_kernel(
    dims,
    video_h, sw_h, bias_ref, tw_h, cot_h,
    out_v, gv_v, gt_v,
    video, cot, sw, tw, wp, wg, xcat, cb, chalo, hb, hpack, hhalo, slope, gpad,
    gtl, rx, ysend, ry, psum, pb, rs, ag,
    load_sem, w_send, w_recv, halo_send, halo_recv, g_send, g_recv, a_send, a_recv,
):
    n_tm, n_clip, height, width, chans, scale = dims
    rows = height * width
    depth = sw_h.shape[1]
    half = rows // 2
    quarter = rows // 4
    chunks = 4
    chunk = half // chunks
    tm = lax.axis_index("tm")
    c = lax.axis_index("clip")

    def flip(value, bit):
        return value + bit - 2 * bit * (lax.rem(value // bit, 2))

    core, ypart = flip(c, 1), flip(c, 2)
    xpart, zpart = flip(tm, 1), flip(tm, 2)
    parity = lax.rem(tm, 2)
    h = lax.rem(tm // 2, 2)

    barrier = pltpu.get_barrier_semaphore()
    for step in range(1, n_tm):
        pl.semaphore_signal(
            barrier, inc=1, device_id=(lax.rem(tm + step, n_tm), c), device_id_type=MESH
        )
    pl.semaphore_signal(barrier, inc=1, device_id=(tm, core), device_id_type=MESH)
    pl.semaphore_signal(barrier, inc=1, device_id=(tm, ypart), device_id_type=MESH)

    loads = [
        pltpu.make_async_copy(sw_h, sw, load_sem.at[0]),
        pltpu.make_async_copy(tw_h, tw, load_sem.at[1]),
        pltpu.make_async_copy(cot_h, cot, load_sem.at[2]),
        pltpu.make_async_copy(video_h, video, load_sem.at[3]),
    ]
    for load in loads:
        load.start()

    def pack(value):
        return jnp.concatenate([value[:quarter], value[quarter:]], axis=1)

    def unpack(ref, slot):
        parts = []
        for q in range(2):
            both = ref[slot, q * quarter : (q + 1) * quarter]
            parts += [both[:, :chans], both[:, chans:]]
        return jnp.concatenate(parts, axis=0)

    loads[0].wait()
    loads[1].wait()
    shard = [sw[tap] for tap in range(9)] + [tw[tap].astype(BF16) for tap in range(3)]
    for pair in range(6):
        wp[c, pair] = jnp.concatenate([shard[2 * pair], shard[2 * pair + 1]], axis=1)
    pl.semaphore_wait(barrier, n_tm + 1)

    def send(src, dst, ssem, rsem, device):
        copy = pltpu.make_async_remote_copy(
            src_ref=src, dst_ref=dst, send_sem=ssem, recv_sem=rsem,
            device_id=device, device_id_type=MESH,
        )
        copy.start()
        return copy

    def wsend(slot, owner, pair, device):
        part = wp.at[owner, pair]
        return send(part, part, w_send.at[slot], w_recv.at[slot], device)

    y_pairs = [2 * h, 2 * h + 1, 4, 5]
    z_pairs = [2 * (1 - h), 2 * (1 - h) + 1]
    y_copies = [wsend(j, c, y_pairs[j], (tm, ypart)) for j in range(4)]
    own_copy = send(wp.at[c], wp.at[c], w_send.at[6], w_recv.at[6], (tm, core))

    loads[2].wait()
    own_cot = cot[...].astype(BF16)
    for q in range(2):
        cb[q * quarter : (q + 1) * quarter] = pack(own_cot[q * half : (q + 1) * half])

    def near_send(base, own, halo, q):
        part = pl.ds(q * chunk, chunk)
        return send(
            own.at[part, :], halo.at[parity, part, :],
            halo_send.at[base + q], halo_recv.at[base + q], (xpart, c),
        )

    def far_copy(base, halo, q):
        target = lax.rem(tm + n_tm + 2 - 4 * parity, n_tm)
        part = pl.ds(q * chunk, chunk)
        return pltpu.make_async_remote_copy(
            src_ref=halo.at[1 - parity, part, :],
            dst_ref=halo.at[parity, part, :],
            send_sem=halo_send.at[base + chunks + q],
            recv_sem=halo_recv.at[base + chunks + q],
            device_id=(target, c),
            device_id_type=MESH,
        )

    sends_far = jnp.logical_or(
        jnp.logical_and(parity == 0, tm + 2 < n_tm), jnp.logical_and(parity == 1, tm >= 2)
    )
    gets_far = jnp.logical_or(
        jnp.logical_and(parity == 0, tm >= 2), jnp.logical_and(parity == 1, tm + 2 < n_tm)
    )

    def far_start(base, halo, q):
        @pl.when(sends_far)
        def _():
            far_copy(base, halo, q).start()

    def far_recv(base, halo):
        @pl.when(gets_far)
        def _():
            for q in range(chunks):
                far_copy(base, halo, q).wait_recv()

    def far_done(base, halo):
        @pl.when(sends_far)
        def _():
            for q in range(chunks):
                far_copy(base, halo, q).wait_send()

    cot_near = [near_send(0, cb, chalo, q) for q in range(chunks)]

    for edge, slot in ((0, 0), (n_tm - 1, 1)):
        @pl.when(tm == edge)
        def _():
            chalo[slot] = jnp.zeros((half, 2 * chans), BF16)
            hhalo[slot] = jnp.zeros((half, 2 * chans), BF16)

    column = lax.rem(lax.broadcasted_iota(jnp.int32, (rows, chans), 0), width)

    def shifted(value, step):
        if step == 0:
            return value
        rolled = pltpu.roll(value, step % rows, 0)
        return jnp.where(column == (0 if step == 1 else width - 1), 0.0, rolled)

    xcat[0:width] = jnp.zeros((width, 3 * chans), BF16)
    xcat[width + rows :] = jnp.zeros((width, 3 * chans), BF16)
    for b in range(3):
        gpad[b, 0:width] = jnp.zeros((width, chans), BF16)
        gpad[b, width + rows :] = jnp.zeros((width, chans), BF16)
    loads[3].wait()
    frame = video[...]
    xcat[width : width + rows] = jnp.concatenate(
        [shifted(frame, 1).astype(BF16), frame.astype(BF16), shifted(frame, -1).astype(BF16)], axis=1
    )

    relays = []
    z_copies = []
    for j in range(2):
        y_copies[j].wait_recv()
        z_copies.append(wsend(4 + j, ypart, y_pairs[j], (zpart, c)))
        relays.append(wsend(7 + j, ypart, y_pairs[j], (tm, core)))
        for q in (2 * j, 2 * j + 1):
            cot_near[q].wait_recv()
            far_start(0, chalo, q)
    y_copies[2].wait_recv()
    relays.append(wsend(9, ypart, y_pairs[2], (tm, core)))
    for j in range(2):
        z_copies[j].wait_recv()
        relays.append(wsend(11 + j, ypart, z_pairs[j], (tm, core)))
    own_copy.wait_recv()
    for copy in relays:
        copy.wait_recv()

    def unpack_weights(pair):
        for owner in range(n_clip):
            both = wp[owner, pair]
            band = slice(owner * depth, (owner + 1) * depth)
            wg[2 * pair, band] = both[:, :chans]
            wg[2 * pair + 1, band] = both[:, chans:]

    for pair in range(5):
        unpack_weights(pair)

    hid_near = []
    for q in range(2):
        acc = bias_ref[...].reshape(1, chans) + jnp.zeros((half, chans), F32)
        for a in range(3):
            acc = acc + nn_dot(
                xcat[a * width + q * half : a * width + (q + 1) * half],
                wg[3 * a : 3 * a + 3].reshape(3 * chans, chans),
            )
        sig = jax.nn.sigmoid(acc)
        hidden = (acc * sig).astype(BF16)
        hb[q * half : (q + 1) * half] = hidden
        hpack[q * quarter : (q + 1) * quarter] = pack(hidden)
        hid_near += [near_send(2 * chunks, hpack, hhalo, 2 * q + e) for e in range(2)]
        slope[q * half : (q + 1) * half] = sig * (1.0 + acc * (1.0 - sig))

    y_copies[3].wait_recv()
    relays.append(wsend(10, ypart, y_pairs[3], (tm, core)))

    lanes = psum.shape[2]
    far_recv(0, chalo)
    hidden_all = hb[...]
    own_cot = cot[...].astype(BF16)
    before, after = unpack(chalo, 0), unpack(chalo, 1)
    products = jnp.concatenate(
        [outer_dot(hidden_all, right) for right in (after, own_cot, before)]
        + [jnp.zeros((chans, n_tm * lanes - 3 * chans), F32)],
        axis=1,
    )
    for owner in range(n_clip):
        gtl[owner % 2, owner // 2] = products[owner * depth : (owner + 1) * depth]
    core_copy = send(
        gtl.at[1 - lax.rem(c, 2)], rx, g_send.at[0], g_recv.at[0], (tm, core)
    )

    def pass_hidden(q):
        hid_near[q].wait_recv()
        far_start(2 * chunks, hhalo, q)

    relays[-1].wait_recv()
    unpack_weights(5)
    grad_h = transpose_dot(after, wg[9]) + transpose_dot(own_cot, wg[10])
    grad_h = grad_h + transpose_dot(before, wg[11])
    pass_hidden(0)

    core_copy.wait_recv()
    yc = c // 2
    mine = lax.rem(c, 2)
    ysend[...] = (gtl[mine, 1 - yc] + rx[1 - yc]).astype(BF16)
    grad_y = send(ysend, ry, g_send.at[1], g_recv.at[1], (tm, ypart))

    grad_s = grad_h * slope[...]
    for b in range(3):
        gpad[b, width : width + rows] = shifted(grad_s, b - 1).astype(BF16)
    pass_hidden(1)
    pass_hidden(2)

    def grad_conv(q):
        acc = cot[q * half : (q + 1) * half]
        for a in range(3):
            start = (2 - a) * width + q * half
            for b in range(3):
                acc = acc + transpose_dot(gpad[b, start : start + half], wg[3 * a + b])
        gv_v[q * half : (q + 1) * half] = acc

    grad_conv(0)
    pass_hidden(3)

    own_sum = gtl[mine, yc] + rx[yc]
    grad_y.wait_recv()
    own_sum = own_sum + ry[...].astype(F32)
    for to in range(n_tm):
        part = own_sum[:, to * lanes : (to + 1) * lanes]
        psum[to] = part
        pb[to] = part.astype(BF16)
    scatters = []
    for step in range(1, n_tm):
        to = lax.rem(tm + step, n_tm)
        scatters.append(
            send(pb.at[to], rs.at[step - 1], a_send.at[step - 1], a_recv.at[step - 1], (to, c))
        )
    grad_conv(1)
    out_v[...] = video[...] + nn_dot(hb[...], wg[10])

    for copy in scatters:
        copy.wait_recv()
    total = psum[tm]
    for step in range(1, n_tm):
        total = total + rs[step - 1].astype(F32)
    ag[tm] = total.astype(BF16)
    gathers = []
    for step in range(1, n_tm):
        to = lax.rem(tm + step, n_tm)
        slot = n_tm - 2 + step
        gathers.append(send(ag.at[tm], ag.at[tm], a_send.at[slot], a_recv.at[slot], (to, c)))

    far_recv(2 * chunks, hhalo)
    out_v[...] = out_v[...] + nn_dot(unpack(hhalo, 0), wg[9]) + nn_dot(unpack(hhalo, 1), wg[11])

    for copy in gathers:
        copy.wait_recv()
    whole = jnp.concatenate([ag[to] for to in range(n_tm)], axis=1).astype(F32) * scale
    for k in range(3):
        gt_v[k] = whole[:, k * chans : (k + 1) * chans]

    for copy in (
        y_copies + z_copies + [own_copy] + relays + cot_near + hid_near
        + [core_copy, grad_y] + scatters + gathers
    ):
        copy.wait_send()
    far_done(0, chalo)
    far_done(2 * chunks, hhalo)


def fused(n_tm, n_clip, video, spatial_w, spatial_b, temporal_w, cotangent):
    clips, frames, height, width, chans = video.shape
    rows = height * width
    depth = spatial_w.shape[1]
    lanes = -(-3 * chans // (128 * n_tm)) * 128
    scale = 1.0 / math.sqrt(rows * n_tm * n_clip)
    any_spec = pl.BlockSpec(memory_space=pltpu.HBM)
    vm_spec = pl.BlockSpec(memory_space=pltpu.VMEM)
    vm = pltpu.VMEM
    dma = pltpu.SemaphoreType.DMA
    out, gv, gt = pl.pallas_call(
        functools.partial(block_kernel, (n_tm, n_clip, height, width, chans, scale)),
        out_shape=(
            jax.ShapeDtypeStruct((rows, chans), F32),
            jax.ShapeDtypeStruct((rows, chans), F32),
            jax.ShapeDtypeStruct((3, depth, chans), F32),
        ),
        in_specs=[any_spec, any_spec, vm_spec, any_spec, any_spec],
        out_specs=(vm_spec, vm_spec, vm_spec),
        scratch_shapes=[
            vm((rows, chans), F32),
            vm((rows, chans), F32),
            vm((9, depth, chans), BF16),
            vm((3, depth, chans), F32),
            vm((n_clip, 6, depth, 2 * chans), BF16),
            vm((12, chans, chans), BF16),
            vm((rows + 2 * width, 3 * chans), BF16),
            vm((rows // 2, 2 * chans), BF16),
            vm((2, rows // 2, 2 * chans), BF16),
            vm((rows, chans), BF16),
            vm((rows // 2, 2 * chans), BF16),
            vm((2, rows // 2, 2 * chans), BF16),
            vm((rows, chans), F32),
            vm((3, rows + 2 * width, chans), BF16),
            vm((2, 2, depth, n_tm * lanes), F32),
            vm((2, depth, n_tm * lanes), F32),
            vm((depth, n_tm * lanes), BF16),
            vm((depth, n_tm * lanes), BF16),
            vm((n_tm, depth, lanes), F32),
            vm((n_tm, depth, lanes), BF16),
            vm((n_tm - 1, depth, lanes), BF16),
            vm((n_tm, depth, lanes), BF16),
            dma((4,)),
            dma((13,)),
            dma((13,)),
            dma((16,)),
            dma((16,)),
            dma((2,)),
            dma((2,)),
            dma((2 * n_tm - 2,)),
            dma((2 * n_tm - 2,)),
        ],
        compiler_params=pltpu.CompilerParams(
            collective_id=0, has_side_effects=True, vmem_limit_bytes=40 * 2**20
        ),
        name="block",
    )(
        video.reshape(rows, chans), spatial_w, spatial_b, temporal_w,
        cotangent.reshape(rows, chans),
    )
    return out.reshape(video.shape), gv.reshape(video.shape), gt


def padded_2(cells, sides, width):
    for axis, dim in sides:
        count = lax.axis_size(axis)
        ends = count - 1
        head = lax.slice_in_dim(cells, 0, width, axis=dim)
        tail = lax.slice_in_dim(cells, cells.shape[dim] - width, cells.shape[dim], axis=dim)
        cells = jnp.concatenate(
            [
                lax.ppermute(tail, axis, [(i, (i + 1) % count) for i in range(ends)]),
                cells,
                lax.ppermute(head, axis, [((i + 1) % count, i) for i in range(ends)]),
            ],
            axis=dim,
        )
    return cells


def native(video, spatial_w, spatial_b, temporal_w, cotangent):
    clips, frames, height, width, chans = video.shape
    row_count = clips * frames * height * width
    pads = ((0, 0), (0, 0), (1, 1), (1, 1), (0, 0))
    padded = jnp.pad(video.astype(BF16), pads)
    temporal_b = temporal_w.astype(BF16)
    spatial_all = lax.all_gather(spatial_w, "clip", axis=1, tiled=True)
    temporal_all = lax.all_gather(temporal_b, "clip", axis=1, tiled=True)
    spatial = jnp.zeros((row_count, chans), F32)
    for y in range(3):
        for x in range(3):
            window = padded[:, :, y : y + height, x : x + width, :].reshape(row_count, chans)
            spatial = spatial + nn_dot(window, spatial_all[3 * y + x])
    spatial = spatial + spatial_b
    sigmoid_s = jax.nn.sigmoid(spatial)
    hidden = (spatial * sigmoid_s).astype(BF16).reshape(video.shape)
    hidden_pad = padded_2(hidden, (("tm", 1),), 1)
    cot_b = cotangent.astype(BF16)
    cot_flat = cot_b.reshape(row_count, chans)
    cot_pad = padded_2(cot_b, (("tm", 1),), 1)
    temporal = jnp.zeros((row_count, chans), F32)
    grad_hidden = jnp.zeros((row_count, chans), F32)
    grads = []
    for k in range(3):
        shifted_hid = hidden_pad[:, k : k + frames].reshape(row_count, chans)
        temporal = temporal + nn_dot(shifted_hid, temporal_all[k])
        shifted_cot = cot_pad[:, 2 - k : 2 - k + frames].reshape(row_count, chans)
        grad_hidden = grad_hidden + transpose_dot(shifted_cot, temporal_all[k])
        grads.append(outer_dot(shifted_hid, cot_flat))
    total_rows = row_count * lax.axis_size("tm") * lax.axis_size("clip")
    summed = lax.psum(jnp.stack(grads), "tm")
    owned = lax.psum_scatter(summed, "clip", scatter_dimension=1, tiled=True)
    grad_spatial = (grad_hidden * sigmoid_s * (1.0 + spatial * (1.0 - sigmoid_s))).astype(BF16)
    grad_frames = jnp.pad(grad_spatial.reshape(video.shape), pads)
    grad_acc = cotangent.reshape(row_count, chans)
    for y in range(3):
        for x in range(3):
            window = grad_frames[:, :, 2 - y : 2 - y + height, 2 - x : 2 - x + width, :]
            window = window.reshape(row_count, chans)
            grad_acc = grad_acc + transpose_dot(window, spatial_all[3 * y + x])
    return (
        video + temporal.reshape(video.shape),
        grad_acc.reshape(video.shape),
        owned * (1.0 / math.sqrt(total_rows)),
    )


def solution(mesh):
    n_tm, n_clip = mesh.shape["tm"], mesh.shape["clip"]

    def on_device(video, spatial_w, spatial_b, temporal_w, cotangent):
        args = (video, spatial_w, spatial_b, temporal_w, cotangent)
        one_frame = video.shape[0] == 1 and video.shape[1] == 1
        if one_frame and spatial_w.shape[1] % 16 == 0 and n_clip == 4 and n_tm % 4 == 0:
            return fused(n_tm, n_clip, *args)
        return native(*args)

    return jax.shard_map(
        on_device,
        mesh=mesh,
        in_specs=(
            P("clip", "tm", None, None, None),
            P(None, "clip", None),
            P(),
            P(None, "clip", None),
            P("clip", "tm", None, None, None),
        ),
        out_specs=(
            P("clip", "tm", None, None, None),
            P("clip", "tm", None, None, None),
            P(None, "clip", None),
        ),
        check_vma=False,
    )
```

```python
import functools
import math

import jax
import jax.numpy as jnp
from jax import lax
from jax.experimental import pallas as pl
from jax.experimental.pallas import tpu as pltpu
from jax.sharding import PartitionSpec as P

F32 = jnp.float32
BF16 = jnp.bfloat16
MESH = pl.DeviceIdType.MESH


def nn_dot(left, right):
    return lax.dot_general(left, right, (((1,), (0,)), ((), ())), preferred_element_type=F32)


def outer_dot(left, right):
    return lax.dot_general(left, right, (((0,), (0,)), ((), ())), preferred_element_type=F32)


def transpose_dot(left, right):
    return lax.dot_general(left, right, (((1,), (1,)), ((), ())), preferred_element_type=F32)


def block_kernel(
    dims,
    video_h, sw_h, bias_ref, tw_h, cot_h,
    out_h, gv_h, gt_h,
    video, cot, sw, tw, wp, wg, xcat, cb, chalo, hb, hpack, hhalo, slope, gpad,
    out_v, gv_v, gt_v, gtl, rx, ysend, ry, psum, pb, rs, ag,
    load_sem, out_sem, w_send, w_recv, halo_send, halo_recv, g_send, g_recv, a_send, a_recv,
):
    n_tm, n_clip, height, width, chans, scale = dims
    rows = height * width
    depth = sw_h.shape[1]
    half = rows // 2
    quarter = rows // 4
    chunks = 4
    chunk = half // chunks
    tm = lax.axis_index("tm")
    c = lax.axis_index("clip")

    def flip(value, bit):
        return value + bit - 2 * bit * (lax.rem(value // bit, 2))

    core, ypart = flip(c, 1), flip(c, 2)
    xpart, zpart = flip(tm, 1), flip(tm, 2)
    parity = lax.rem(tm, 2)
    h = lax.rem(tm // 2, 2)

    barrier = pltpu.get_barrier_semaphore()
    for step in range(1, n_tm):
        pl.semaphore_signal(
            barrier, inc=1, device_id=(lax.rem(tm + step, n_tm), c), device_id_type=MESH
        )
    pl.semaphore_signal(barrier, inc=1, device_id=(tm, core), device_id_type=MESH)
    pl.semaphore_signal(barrier, inc=1, device_id=(tm, ypart), device_id_type=MESH)

    loads = [
        pltpu.make_async_copy(sw_h, sw, load_sem.at[0]),
        pltpu.make_async_copy(tw_h, tw, load_sem.at[1]),
        pltpu.make_async_copy(cot_h, cot, load_sem.at[2]),
        pltpu.make_async_copy(video_h, video, load_sem.at[3]),
    ]
    for load in loads:
        load.start()

    def pack(value):
        return jnp.concatenate([value[:quarter], value[quarter:]], axis=1)

    def unpack(ref, slot):
        parts = []
        for q in range(2):
            both = ref[slot, q * quarter : (q + 1) * quarter]
            parts += [both[:, :chans], both[:, chans:]]
        return jnp.concatenate(parts, axis=0)

    loads[0].wait()
    loads[1].wait()
    shard = [sw[tap] for tap in range(9)] + [tw[tap].astype(BF16) for tap in range(3)]
    for pair in range(6):
        wp[c, pair] = jnp.concatenate([shard[2 * pair], shard[2 * pair + 1]], axis=1)
    pl.semaphore_wait(barrier, n_tm + 1)

    def send(src, dst, ssem, rsem, device):
        copy = pltpu.make_async_remote_copy(
            src_ref=src, dst_ref=dst, send_sem=ssem, recv_sem=rsem,
            device_id=device, device_id_type=MESH,
        )
        copy.start()
        return copy

    def wsend(slot, owner, pair, device):
        part = wp.at[owner, pair]
        return send(part, part, w_send.at[slot], w_recv.at[slot], device)

    y_pairs = [2 * h, 2 * h + 1, 4, 5]
    z_pairs = [2 * (1 - h), 2 * (1 - h) + 1]
    y_copies = [wsend(j, c, y_pairs[j], (tm, ypart)) for j in range(4)]
    own_copy = send(wp.at[c], wp.at[c], w_send.at[6], w_recv.at[6], (tm, core))

    loads[2].wait()
    own_cot = cot[...].astype(BF16)
    for q in range(2):
        cb[q * quarter : (q + 1) * quarter] = pack(own_cot[q * half : (q + 1) * half])

    def near_send(base, own, halo, q):
        part = pl.ds(q * chunk, chunk)
        return send(
            own.at[part, :], halo.at[parity, part, :],
            halo_send.at[base + q], halo_recv.at[base + q], (xpart, c),
        )

    def far_copy(base, halo, q):
        target = lax.rem(tm + n_tm + 2 - 4 * parity, n_tm)
        part = pl.ds(q * chunk, chunk)
        return pltpu.make_async_remote_copy(
            src_ref=halo.at[1 - parity, part, :],
            dst_ref=halo.at[parity, part, :],
            send_sem=halo_send.at[base + chunks + q],
            recv_sem=halo_recv.at[base + chunks + q],
            device_id=(target, c),
            device_id_type=MESH,
        )

    sends_far = jnp.logical_or(
        jnp.logical_and(parity == 0, tm + 2 < n_tm), jnp.logical_and(parity == 1, tm >= 2)
    )
    gets_far = jnp.logical_or(
        jnp.logical_and(parity == 0, tm >= 2), jnp.logical_and(parity == 1, tm + 2 < n_tm)
    )

    def far_start(base, halo, q):
        @pl.when(sends_far)
        def _():
            far_copy(base, halo, q).start()

    def far_recv(base, halo):
        @pl.when(gets_far)
        def _():
            for q in range(chunks):
                far_copy(base, halo, q).wait_recv()

    def far_done(base, halo):
        @pl.when(sends_far)
        def _():
            for q in range(chunks):
                far_copy(base, halo, q).wait_send()

    cot_near = [near_send(0, cb, chalo, q) for q in range(chunks)]

    for edge, slot in ((0, 0), (n_tm - 1, 1)):
        @pl.when(tm == edge)
        def _():
            chalo[slot] = jnp.zeros((half, 2 * chans), BF16)
            hhalo[slot] = jnp.zeros((half, 2 * chans), BF16)

    column = lax.rem(lax.broadcasted_iota(jnp.int32, (rows, chans), 0), width)

    def shifted(value, step):
        if step == 0:
            return value
        rolled = pltpu.roll(value, step % rows, 0)
        return jnp.where(column == (0 if step == 1 else width - 1), 0.0, rolled)

    xcat[0:width] = jnp.zeros((width, 3 * chans), BF16)
    xcat[width + rows :] = jnp.zeros((width, 3 * chans), BF16)
    for b in range(3):
        gpad[b, 0:width] = jnp.zeros((width, chans), BF16)
        gpad[b, width + rows :] = jnp.zeros((width, chans), BF16)
    loads[3].wait()
    frame = video[...]
    xcat[width : width + rows] = jnp.concatenate(
        [shifted(frame, 1).astype(BF16), frame.astype(BF16), shifted(frame, -1).astype(BF16)], axis=1
    )

    relays = []
    z_copies = []
    for j in range(2):
        y_copies[j].wait_recv()
        z_copies.append(wsend(4 + j, ypart, y_pairs[j], (zpart, c)))
        relays.append(wsend(7 + j, ypart, y_pairs[j], (tm, core)))
        for q in (2 * j, 2 * j + 1):
            cot_near[q].wait_recv()
            far_start(0, chalo, q)
    y_copies[2].wait_recv()
    relays.append(wsend(9, ypart, y_pairs[2], (tm, core)))
    for j in range(2):
        z_copies[j].wait_recv()
        relays.append(wsend(11 + j, ypart, z_pairs[j], (tm, core)))
    own_copy.wait_recv()
    for copy in relays:
        copy.wait_recv()

    def unpack_weights(pair):
        for owner in range(n_clip):
            both = wp[owner, pair]
            band = slice(owner * depth, (owner + 1) * depth)
            wg[2 * pair, band] = both[:, :chans]
            wg[2 * pair + 1, band] = both[:, chans:]

    for pair in range(5):
        unpack_weights(pair)

    hid_near = []
    for q in range(2):
        acc = bias_ref[...].reshape(1, chans) + jnp.zeros((half, chans), F32)
        for a in range(3):
            acc = acc + nn_dot(
                xcat[a * width + q * half : a * width + (q + 1) * half],
                wg[3 * a : 3 * a + 3].reshape(3 * chans, chans),
            )
        sig = jax.nn.sigmoid(acc)
        hidden = (acc * sig).astype(BF16)
        hb[q * half : (q + 1) * half] = hidden
        hpack[q * quarter : (q + 1) * quarter] = pack(hidden)
        hid_near += [near_send(2 * chunks, hpack, hhalo, 2 * q + e) for e in range(2)]
        slope[q * half : (q + 1) * half] = sig * (1.0 + acc * (1.0 - sig))

    y_copies[3].wait_recv()
    relays.append(wsend(10, ypart, y_pairs[3], (tm, core)))

    lanes = psum.shape[2]
    far_recv(0, chalo)
    hidden_all = hb[...]
    own_cot = cot[...].astype(BF16)
    before, after = unpack(chalo, 0), unpack(chalo, 1)
    products = jnp.concatenate(
        [outer_dot(hidden_all, right) for right in (after, own_cot, before)]
        + [jnp.zeros((chans, n_tm * lanes - 3 * chans), F32)],
        axis=1,
    )
    for owner in range(n_clip):
        gtl[owner % 2, owner // 2] = products[owner * depth : (owner + 1) * depth]
    yc = c // 2
    mine = lax.rem(c, 2)
    core_copies = [
        send(gtl.at[1 - mine, side], rx.at[side], g_send.at[e], g_recv.at[e], (tm, core))
        for e, side in enumerate((1 - yc, yc))
    ]

    def pass_hidden(q):
        hid_near[q].wait_recv()
        far_start(2 * chunks, hhalo, q)

    relays[-1].wait_recv()
    unpack_weights(5)
    grad_h = transpose_dot(after, wg[9]) + transpose_dot(own_cot, wg[10])
    grad_h = grad_h + transpose_dot(before, wg[11])
    pass_hidden(0)

    core_copies[0].wait_recv()
    ysend[...] = (gtl[mine, 1 - yc] + rx[1 - yc]).astype(BF16)
    grad_y = send(ysend, ry, g_send.at[2], g_recv.at[2], (tm, ypart))

    grad_s = grad_h * slope[...]
    for b in range(3):
        gpad[b, width : width + rows] = shifted(grad_s, b - 1).astype(BF16)
    pass_hidden(1)
    pass_hidden(2)

    def grad_conv(q):
        acc = cot[q * half : (q + 1) * half]
        for a in range(3):
            start = (2 - a) * width + q * half
            for b in range(3):
                acc = acc + transpose_dot(gpad[b, start : start + half], wg[3 * a + b])
        gv_v[q * half : (q + 1) * half] = acc

    grad_conv(0)
    pass_hidden(3)

    core_copies[1].wait_recv()
    own_sum = gtl[mine, yc] + rx[yc]
    grad_y.wait_recv()
    own_sum = own_sum + ry[...].astype(F32)
    for to in range(n_tm):
        part = own_sum[:, to * lanes : (to + 1) * lanes]
        psum[to] = part
        pb[to] = part.astype(BF16)
    order = sorted(range(1, n_tm), key=lambda step: -min(step, n_tm - step))
    scatters = []
    for step in order:
        to = lax.rem(tm + step, n_tm)
        scatters.append(
            send(pb.at[to], rs.at[step - 1], a_send.at[step - 1], a_recv.at[step - 1], (to, c))
        )
    grad_conv(1)
    gv_out = pltpu.make_async_copy(gv_v, gv_h, out_sem.at[0])
    gv_out.start()
    out_v[...] = video[...] + nn_dot(hb[...], wg[10])

    for copy in scatters:
        copy.wait_recv()
    total = psum[tm]
    for step in range(1, n_tm):
        total = total + rs[step - 1].astype(F32)
    ag[tm] = total.astype(BF16)
    gathers = []
    for step in order:
        to = lax.rem(tm + step, n_tm)
        slot = n_tm - 2 + step
        gathers.append(send(ag.at[tm], ag.at[tm], a_send.at[slot], a_recv.at[slot], (to, c)))

    far_recv(2 * chunks, hhalo)
    out_v[...] = out_v[...] + nn_dot(unpack(hhalo, 0), wg[9]) + nn_dot(unpack(hhalo, 1), wg[11])
    out_out = pltpu.make_async_copy(out_v, out_h, out_sem.at[1])
    out_out.start()

    for copy in gathers:
        copy.wait_recv()
    whole = jnp.concatenate([ag[to] for to in range(n_tm)], axis=1).astype(F32) * scale
    for k in range(3):
        gt_v[k] = whole[:, k * chans : (k + 1) * chans]
    gt_out = pltpu.make_async_copy(gt_v, gt_h, out_sem.at[2])
    gt_out.start()

    for copy in (
        y_copies + z_copies + [own_copy] + relays + cot_near + hid_near
        + core_copies + [grad_y] + scatters + gathers
    ):
        copy.wait_send()
    far_done(0, chalo)
    far_done(2 * chunks, hhalo)
    gv_out.wait()
    out_out.wait()
    gt_out.wait()


def hand_over(*refs):
    n = (len(refs) - 2) // 3
    ins, outs, held, (sem_in, sem_out) = refs[:n], refs[n : 2 * n], refs[2 * n : 3 * n], refs[3 * n :]
    reads = [pltpu.make_async_copy(ins[e], held[e], sem_in.at[e]) for e in range(n)]
    writes = [pltpu.make_async_copy(held[e], outs[e], sem_out.at[e]) for e in range(n)]
    for read in reads:
        read.start()
    for read, write in zip(reads, writes):
        read.wait()
        write.start()
    for write in writes:
        write.wait()


def fused(n_tm, n_clip, video, spatial_w, spatial_b, temporal_w, cotangent):
    clips, frames, height, width, chans = video.shape
    rows = height * width
    depth = spatial_w.shape[1]
    lanes = -(-3 * chans // (128 * n_tm)) * 128
    scale = 1.0 / math.sqrt(rows * n_tm * n_clip)
    any_spec = pl.BlockSpec(memory_space=pltpu.HBM)
    vm_spec = pl.BlockSpec(memory_space=pltpu.VMEM)
    vm = pltpu.VMEM
    dma = pltpu.SemaphoreType.DMA
    results = pl.pallas_call(
        functools.partial(block_kernel, (n_tm, n_clip, height, width, chans, scale)),
        out_shape=(
            jax.ShapeDtypeStruct((rows, chans), F32),
            jax.ShapeDtypeStruct((rows, chans), F32),
            jax.ShapeDtypeStruct((3, depth, chans), F32),
        ),
        in_specs=[any_spec, any_spec, vm_spec, any_spec, any_spec],
        out_specs=(any_spec, any_spec, any_spec),
        scratch_shapes=[
            vm((rows, chans), F32),
            vm((rows, chans), F32),
            vm((9, depth, chans), BF16),
            vm((3, depth, chans), F32),
            vm((n_clip, 6, depth, 2 * chans), BF16),
            vm((12, chans, chans), BF16),
            vm((rows + 2 * width, 3 * chans), BF16),
            vm((rows // 2, 2 * chans), BF16),
            vm((2, rows // 2, 2 * chans), BF16),
            vm((rows, chans), BF16),
            vm((rows // 2, 2 * chans), BF16),
            vm((2, rows // 2, 2 * chans), BF16),
            vm((rows, chans), F32),
            vm((3, rows + 2 * width, chans), BF16),
            vm((rows, chans), F32),
            vm((rows, chans), F32),
            vm((3, depth, chans), F32),
            vm((2, 2, depth, n_tm * lanes), F32),
            vm((2, depth, n_tm * lanes), F32),
            vm((depth, n_tm * lanes), BF16),
            vm((depth, n_tm * lanes), BF16),
            vm((n_tm, depth, lanes), F32),
            vm((n_tm, depth, lanes), BF16),
            vm((n_tm - 1, depth, lanes), BF16),
            vm((n_tm, depth, lanes), BF16),
            dma((4,)),
            dma((3,)),
            dma((13,)),
            dma((13,)),
            dma((16,)),
            dma((16,)),
            dma((3,)),
            dma((3,)),
            dma((2 * n_tm - 2,)),
            dma((2 * n_tm - 2,)),
        ],
        compiler_params=pltpu.CompilerParams(
            collective_id=0, has_side_effects=True, vmem_limit_bytes=62 * 2**20
        ),
        name="block",
    )(
        video.reshape(rows, chans), spatial_w, spatial_b, temporal_w,
        cotangent.reshape(rows, chans),
    )
    shapes = tuple(jax.ShapeDtypeStruct(array.shape, F32) for array in results)
    out, gv, gt = pl.pallas_call(
        hand_over,
        out_shape=shapes,
        in_specs=[any_spec] * 3,
        out_specs=(any_spec,) * 3,
        scratch_shapes=[vm(shape.shape, F32) for shape in shapes] + [dma((3,)), dma((3,))],
        compiler_params=pltpu.CompilerParams(vmem_limit_bytes=62 * 2**20),
        name="hand_over",
    )(*results)
    return out.reshape(video.shape), gv.reshape(video.shape), gt


def padded_2(cells, sides, width):
    for axis, dim in sides:
        count = lax.axis_size(axis)
        ends = count - 1
        head = lax.slice_in_dim(cells, 0, width, axis=dim)
        tail = lax.slice_in_dim(cells, cells.shape[dim] - width, cells.shape[dim], axis=dim)
        cells = jnp.concatenate(
            [
                lax.ppermute(tail, axis, [(i, (i + 1) % count) for i in range(ends)]),
                cells,
                lax.ppermute(head, axis, [((i + 1) % count, i) for i in range(ends)]),
            ],
            axis=dim,
        )
    return cells


def native(video, spatial_w, spatial_b, temporal_w, cotangent):
    clips, frames, height, width, chans = video.shape
    row_count = clips * frames * height * width
    pads = ((0, 0), (0, 0), (1, 1), (1, 1), (0, 0))
    padded = jnp.pad(video.astype(BF16), pads)
    temporal_b = temporal_w.astype(BF16)
    spatial_all = lax.all_gather(spatial_w, "clip", axis=1, tiled=True)
    temporal_all = lax.all_gather(temporal_b, "clip", axis=1, tiled=True)
    spatial = jnp.zeros((row_count, chans), F32)
    for y in range(3):
        for x in range(3):
            window = padded[:, :, y : y + height, x : x + width, :].reshape(row_count, chans)
            spatial = spatial + nn_dot(window, spatial_all[3 * y + x])
    spatial = spatial + spatial_b
    sigmoid_s = jax.nn.sigmoid(spatial)
    hidden = (spatial * sigmoid_s).astype(BF16).reshape(video.shape)
    hidden_pad = padded_2(hidden, (("tm", 1),), 1)
    cot_b = cotangent.astype(BF16)
    cot_flat = cot_b.reshape(row_count, chans)
    cot_pad = padded_2(cot_b, (("tm", 1),), 1)
    temporal = jnp.zeros((row_count, chans), F32)
    grad_hidden = jnp.zeros((row_count, chans), F32)
    grads = []
    for k in range(3):
        shifted_hid = hidden_pad[:, k : k + frames].reshape(row_count, chans)
        temporal = temporal + nn_dot(shifted_hid, temporal_all[k])
        shifted_cot = cot_pad[:, 2 - k : 2 - k + frames].reshape(row_count, chans)
        grad_hidden = grad_hidden + transpose_dot(shifted_cot, temporal_all[k])
        grads.append(outer_dot(shifted_hid, cot_flat))
    total_rows = row_count * lax.axis_size("tm") * lax.axis_size("clip")
    summed = lax.psum(jnp.stack(grads), "tm")
    owned = lax.psum_scatter(summed, "clip", scatter_dimension=1, tiled=True)
    grad_spatial = (grad_hidden * sigmoid_s * (1.0 + spatial * (1.0 - sigmoid_s))).astype(BF16)
    grad_frames = jnp.pad(grad_spatial.reshape(video.shape), pads)
    grad_acc = cotangent.reshape(row_count, chans)
    for y in range(3):
        for x in range(3):
            window = grad_frames[:, :, 2 - y : 2 - y + height, 2 - x : 2 - x + width, :]
            window = window.reshape(row_count, chans)
            grad_acc = grad_acc + transpose_dot(window, spatial_all[3 * y + x])
    return (
        video + temporal.reshape(video.shape),
        grad_acc.reshape(video.shape),
        owned * (1.0 / math.sqrt(total_rows)),
    )


def solution(mesh):
    n_tm, n_clip = mesh.shape["tm"], mesh.shape["clip"]

    def on_device(video, spatial_w, spatial_b, temporal_w, cotangent):
        args = (video, spatial_w, spatial_b, temporal_w, cotangent)
        one_frame = video.shape[0] == 1 and video.shape[1] == 1
        if one_frame and spatial_w.shape[1] % 16 == 0 and n_clip == 4 and n_tm % 4 == 0:
            return fused(n_tm, n_clip, *args)
        return native(*args)

    return jax.shard_map(
        on_device,
        mesh=mesh,
        in_specs=(
            P("clip", "tm", None, None, None),
            P(None, "clip", None),
            P(),
            P(None, "clip", None),
            P("clip", "tm", None, None, None),
        ),
        out_specs=(
            P("clip", "tm", None, None, None),
            P("clip", "tm", None, None, None),
            P(None, "clip", None),
        ),
        check_vma=False,
    )
```

```python
import functools
import math

import jax
import jax.numpy as jnp
from jax import lax
from jax.experimental import pallas as pl
from jax.experimental.pallas import tpu as pltpu
from jax.sharding import PartitionSpec as P

F32 = jnp.float32
BF16 = jnp.bfloat16
MESH = pl.DeviceIdType.MESH


def nn_dot(left, right):
    return lax.dot_general(left, right, (((1,), (0,)), ((), ())), preferred_element_type=F32)


def outer_dot(left, right):
    return lax.dot_general(left, right, (((0,), (0,)), ((), ())), preferred_element_type=F32)


def transpose_dot(left, right):
    return lax.dot_general(left, right, (((1,), (1,)), ((), ())), preferred_element_type=F32)


def block_kernel(
    dims,
    video_h, sw_h, bias_ref, tw_h, cot_h,
    out_h, gv_h, gt_h,
    video, cot, sw, tw, wp, wg, xcat, cb, chalo, hb, hpack, hhalo, slope, gpad,
    out_v, gv_v, gt_v, gtl, rx, ysend, ry, psum, pb, rs, ag,
    load_sem, out_sem, w_send, w_recv, halo_send, halo_recv, g_send, g_recv, a_send, a_recv,
):
    n_tm, n_clip, height, width, chans, scale = dims
    rows = height * width
    depth = sw_h.shape[1]
    half = rows // 2
    quarter = rows // 4
    chunks = 4
    chunk = half // chunks
    tm = lax.axis_index("tm")
    c = lax.axis_index("clip")

    def flip(value, bit):
        return value + bit - 2 * bit * (lax.rem(value // bit, 2))

    core, ypart = flip(c, 1), flip(c, 2)
    xpart, zpart = flip(tm, 1), flip(tm, 2)
    parity = lax.rem(tm, 2)
    h = lax.rem(tm // 2, 2)

    barrier = pltpu.get_barrier_semaphore()
    for step in range(1, n_tm):
        pl.semaphore_signal(
            barrier, inc=1, device_id=(lax.rem(tm + step, n_tm), c), device_id_type=MESH
        )
    pl.semaphore_signal(barrier, inc=1, device_id=(tm, core), device_id_type=MESH)
    pl.semaphore_signal(barrier, inc=1, device_id=(tm, ypart), device_id_type=MESH)

    loads = [
        pltpu.make_async_copy(sw_h, sw, load_sem.at[0]),
        pltpu.make_async_copy(tw_h, tw, load_sem.at[1]),
        pltpu.make_async_copy(cot_h, cot, load_sem.at[2]),
        pltpu.make_async_copy(video_h, video, load_sem.at[3]),
    ]
    for load in loads:
        load.start()

    def pack(value):
        return jnp.concatenate([value[:quarter], value[quarter:]], axis=1)

    def unpack(ref, slot):
        parts = []
        for q in range(2):
            both = ref[slot, q * quarter : (q + 1) * quarter]
            parts += [both[:, :chans], both[:, chans:]]
        return jnp.concatenate(parts, axis=0)

    loads[0].wait()
    loads[1].wait()
    shard = [sw[tap] for tap in range(9)] + [tw[tap].astype(BF16) for tap in range(3)]
    for pair in range(6):
        wp[c, pair] = jnp.concatenate([shard[2 * pair], shard[2 * pair + 1]], axis=1)
    pl.semaphore_wait(barrier, n_tm + 1)

    def send(src, dst, ssem, rsem, device):
        copy = pltpu.make_async_remote_copy(
            src_ref=src, dst_ref=dst, send_sem=ssem, recv_sem=rsem,
            device_id=device, device_id_type=MESH,
        )
        copy.start()
        return copy

    def wsend(slot, owner, pair, device):
        part = wp.at[owner, pair]
        return send(part, part, w_send.at[slot], w_recv.at[slot], device)

    y_pairs = [parity, 2 + h, 4, 5]
    shared_pairs = [1 - parity, 3 - h]
    sharers = [(xpart, c), (zpart, c)]
    y_copies = [wsend(j, c, y_pairs[j], (tm, ypart)) for j in range(4)]
    own_copy = send(wp.at[c], wp.at[c], w_send.at[6], w_recv.at[6], (tm, core))

    loads[2].wait()
    own_cot = cot[...].astype(BF16)
    for q in range(2):
        cb[q * quarter : (q + 1) * quarter] = pack(own_cot[q * half : (q + 1) * half])

    def near_send(base, own, halo, q):
        part = pl.ds(q * chunk, chunk)
        return send(
            own.at[part, :], halo.at[parity, part, :],
            halo_send.at[base + q], halo_recv.at[base + q], (xpart, c),
        )

    def far_copy(base, halo, q):
        target = lax.rem(tm + n_tm + 2 - 4 * parity, n_tm)
        part = pl.ds(q * chunk, chunk)
        return pltpu.make_async_remote_copy(
            src_ref=halo.at[1 - parity, part, :],
            dst_ref=halo.at[parity, part, :],
            send_sem=halo_send.at[base + chunks + q],
            recv_sem=halo_recv.at[base + chunks + q],
            device_id=(target, c),
            device_id_type=MESH,
        )

    sends_far = jnp.logical_or(
        jnp.logical_and(parity == 0, tm + 2 < n_tm), jnp.logical_and(parity == 1, tm >= 2)
    )
    gets_far = jnp.logical_or(
        jnp.logical_and(parity == 0, tm >= 2), jnp.logical_and(parity == 1, tm + 2 < n_tm)
    )

    def far_start(base, halo, q):
        @pl.when(sends_far)
        def _():
            far_copy(base, halo, q).start()

    def far_recv(base, halo):
        @pl.when(gets_far)
        def _():
            for q in range(chunks):
                far_copy(base, halo, q).wait_recv()

    def far_done(base, halo):
        @pl.when(sends_far)
        def _():
            for q in range(chunks):
                far_copy(base, halo, q).wait_send()

    cot_near = [near_send(0, cb, chalo, q) for q in range(2)]

    for edge, slot in ((0, 0), (n_tm - 1, 1)):
        @pl.when(tm == edge)
        def _():
            chalo[slot] = jnp.zeros((half, 2 * chans), BF16)
            hhalo[slot] = jnp.zeros((half, 2 * chans), BF16)

    column = lax.rem(lax.broadcasted_iota(jnp.int32, (rows, chans), 0), width)

    def shifted(value, step):
        if step == 0:
            return value
        rolled = pltpu.roll(value, step % rows, 0)
        return jnp.where(column == (0 if step == 1 else width - 1), 0.0, rolled)

    xcat[0:width] = jnp.zeros((width, 3 * chans), BF16)
    xcat[width + rows :] = jnp.zeros((width, 3 * chans), BF16)
    for b in range(3):
        gpad[b, 0:width] = jnp.zeros((width, chans), BF16)
        gpad[b, width + rows :] = jnp.zeros((width, chans), BF16)
    loads[3].wait()
    frame = video[...]
    xcat[width : width + rows] = jnp.concatenate(
        [shifted(frame, 1).astype(BF16), frame.astype(BF16), shifted(frame, -1).astype(BF16)], axis=1
    )

    relays = []
    z_copies = []
    for j in range(2):
        y_copies[j].wait_recv()
        z_copies.append(wsend(4 + j, ypart, y_pairs[j], sharers[j]))
        if j == 0:
            cot_near += [near_send(0, cb, chalo, q) for q in range(2, chunks)]
        relays.append(wsend(7 + j, ypart, y_pairs[j], (tm, core)))
        cot_near[j].wait_recv()
        far_start(0, chalo, j)
    y_copies[2].wait_recv()
    relays.append(wsend(9, ypart, y_pairs[2], (tm, core)))
    for j in range(2):
        z_copies[j].wait_recv()
        relays.append(wsend(11 + j, ypart, shared_pairs[j], (tm, core)))
        cot_near[2 + j].wait_recv()
        far_start(0, chalo, 2 + j)
    own_copy.wait_recv()
    for copy in relays:
        copy.wait_recv()

    def unpack_weights(pair):
        for owner in range(n_clip):
            both = wp[owner, pair]
            band = slice(owner * depth, (owner + 1) * depth)
            wg[2 * pair, band] = both[:, :chans]
            wg[2 * pair + 1, band] = both[:, chans:]

    for pair in range(5):
        unpack_weights(pair)

    hid_near = []
    for q in range(2):
        acc = bias_ref[...].reshape(1, chans) + jnp.zeros((half, chans), F32)
        for a in range(3):
            acc = acc + nn_dot(
                xcat[a * width + q * half : a * width + (q + 1) * half],
                wg[3 * a : 3 * a + 3].reshape(3 * chans, chans),
            )
        sig = jax.nn.sigmoid(acc)
        hidden = (acc * sig).astype(BF16)
        hb[q * half : (q + 1) * half] = hidden
        hpack[q * quarter : (q + 1) * quarter] = pack(hidden)
        hid_near += [near_send(2 * chunks, hpack, hhalo, 2 * q + e) for e in range(2)]
        slope[q * half : (q + 1) * half] = sig * (1.0 + acc * (1.0 - sig))

    y_copies[3].wait_recv()
    relays.append(wsend(10, ypart, y_pairs[3], (tm, core)))

    lanes = psum.shape[2]
    wide = n_tm // 2 * lanes
    far_recv(0, chalo)
    hidden_all = hb[...]
    own_cot = cot[...].astype(BF16)
    before, after = unpack(chalo, 0), unpack(chalo, 1)
    products = jnp.concatenate(
        [outer_dot(hidden_all, right) for right in (after, own_cot, before)]
        + [jnp.zeros((chans, n_tm * lanes - 3 * chans), F32)],
        axis=1,
    )
    for owner in range(n_clip):
        gtl[owner % 2, owner // 2] = products[owner * depth : (owner + 1) * depth]
    yc = c // 2
    mine = lax.rem(c, 2)
    core_copies = [
        send(gtl.at[1 - mine, side], rx.at[side], g_send.at[e], g_recv.at[e], (tm, core))
        for e, side in enumerate((1 - yc, yc))
    ]

    def pass_hidden(q):
        hid_near[q].wait_recv()
        far_start(2 * chunks, hhalo, q)

    relays[-1].wait_recv()
    unpack_weights(5)
    grad_h = transpose_dot(after, wg[9]) + transpose_dot(own_cot, wg[10])
    grad_h = grad_h + transpose_dot(before, wg[11])
    pass_hidden(0)

    core_copies[0].wait_recv()
    y_sum = (gtl[mine, 1 - yc] + rx[1 - yc]).astype(BF16)
    grad_y = []
    for e in range(2):
        ysend[e] = y_sum[:, e * wide : (e + 1) * wide]
        grad_y.append(send(ysend.at[e], ry.at[e], g_send.at[2 + e], g_recv.at[2 + e], (tm, ypart)))

    grad_s = grad_h * slope[...]
    for b in range(3):
        gpad[b, width : width + rows] = shifted(grad_s, b - 1).astype(BF16)
    pass_hidden(1)
    pass_hidden(2)

    def grad_conv(q):
        acc = cot[q * half : (q + 1) * half]
        for a in range(3):
            start = (2 - a) * width + q * half
            for b in range(3):
                acc = acc + transpose_dot(gpad[b, start : start + half], wg[3 * a + b])
        gv_v[q * half : (q + 1) * half] = acc

    grad_conv(0)
    pass_hidden(3)

    core_copies[1].wait_recv()
    own_sum = gtl[mine, yc] + rx[yc]
    def scatter_copy(to):
        return pltpu.make_async_remote_copy(
            src_ref=pb.at[to], dst_ref=rs.at[tm], send_sem=a_send.at[to], recv_sem=a_recv.at[tm],
            device_id=(to, c), device_id_type=MESH,
        )

    def arrival(sender):
        return pltpu.make_async_remote_copy(
            src_ref=pb.at[sender], dst_ref=rs.at[sender], send_sem=a_send.at[sender],
            recv_sem=a_recv.at[sender], device_id=(sender, c), device_id_type=MESH,
        )

    for e in range(2):
        grad_y[e].wait_recv()
        both = own_sum[:, e * wide : (e + 1) * wide] + ry[e].astype(F32)
        for place in range(n_tm // 2):
            to = e * (n_tm // 2) + place
            part = both[:, place * lanes : (place + 1) * lanes]
            psum[to] = part
            pb[to] = part.astype(BF16)

            @pl.when(tm != to)
            def _():
                scatter_copy(to).start()

    grad_conv(1)
    gv_out = pltpu.make_async_copy(gv_v, gv_h, out_sem.at[0])
    gv_out.start()
    out_v[...] = video[...] + nn_dot(hb[...], wg[10])

    rs[tm] = jnp.zeros(rs.shape[1:], BF16)
    for sender in range(n_tm):
        @pl.when(tm != sender)
        def _():
            arrival(sender).wait_recv()
    total = psum[tm]
    for sender in range(n_tm):
        total = total + rs[sender].astype(F32)
    ag[tm] = total.astype(BF16)
    order = sorted(range(1, n_tm), key=lambda step: -min(step, n_tm - step))
    gathers = []
    for step in order:
        to = lax.rem(tm + step, n_tm)
        slot = n_tm - 1 + step
        gathers.append(send(ag.at[tm], ag.at[tm], a_send.at[slot], a_recv.at[slot], (to, c)))

    far_recv(2 * chunks, hhalo)
    out_v[...] = out_v[...] + nn_dot(unpack(hhalo, 0), wg[9]) + nn_dot(unpack(hhalo, 1), wg[11])
    out_out = pltpu.make_async_copy(out_v, out_h, out_sem.at[1])
    out_out.start()

    for copy in gathers:
        copy.wait_recv()
    whole = jnp.concatenate([ag[to] for to in range(n_tm)], axis=1).astype(F32) * scale
    for k in range(3):
        gt_v[k] = whole[:, k * chans : (k + 1) * chans]
    gt_out = pltpu.make_async_copy(gt_v, gt_h, out_sem.at[2])
    gt_out.start()

    for copy in (
        y_copies + z_copies + [own_copy] + relays + cot_near + hid_near
        + core_copies + grad_y + gathers
    ):
        copy.wait_send()
    far_done(0, chalo)
    far_done(2 * chunks, hhalo)
    for to in range(n_tm):
        @pl.when(tm != to)
        def _():
            arrival(to).wait_send()
    gv_out.wait()
    out_out.wait()
    gt_out.wait()


def hand_over(*refs):
    n = (len(refs) - 2) // 3
    ins, outs, held, (sem_in, sem_out) = refs[:n], refs[n : 2 * n], refs[2 * n : 3 * n], refs[3 * n :]
    reads, writes = [], []
    for e in range(n):
        extent = ins[e].shape[0]
        count = 4 if extent % 64 == 0 else 1
        for q in range(count):
            part = pl.ds(q * (extent // count), extent // count)
            slot = 4 * e + q
            reads.append(pltpu.make_async_copy(ins[e].at[part], held[e].at[part], sem_in.at[slot]))
            writes.append(pltpu.make_async_copy(held[e].at[part], outs[e].at[part], sem_out.at[slot]))
    for read in reads:
        read.start()
    for read, write in zip(reads, writes):
        read.wait()
        write.start()
    for write in writes:
        write.wait()


def fused(n_tm, n_clip, video, spatial_w, spatial_b, temporal_w, cotangent):
    clips, frames, height, width, chans = video.shape
    rows = height * width
    depth = spatial_w.shape[1]
    lanes = -(-3 * chans // (128 * n_tm)) * 128
    scale = 1.0 / math.sqrt(rows * n_tm * n_clip)
    any_spec = pl.BlockSpec(memory_space=pltpu.HBM)
    vm_spec = pl.BlockSpec(memory_space=pltpu.VMEM)
    vm = pltpu.VMEM
    dma = pltpu.SemaphoreType.DMA
    results = pl.pallas_call(
        functools.partial(block_kernel, (n_tm, n_clip, height, width, chans, scale)),
        out_shape=(
            jax.ShapeDtypeStruct((rows, chans), F32),
            jax.ShapeDtypeStruct((rows, chans), F32),
            jax.ShapeDtypeStruct((3, depth, chans), F32),
        ),
        in_specs=[any_spec, any_spec, vm_spec, any_spec, any_spec],
        out_specs=(any_spec, any_spec, any_spec),
        scratch_shapes=[
            vm((rows, chans), F32),
            vm((rows, chans), F32),
            vm((9, depth, chans), BF16),
            vm((3, depth, chans), F32),
            vm((n_clip, 6, depth, 2 * chans), BF16),
            vm((12, chans, chans), BF16),
            vm((rows + 2 * width, 3 * chans), BF16),
            vm((rows // 2, 2 * chans), BF16),
            vm((2, rows // 2, 2 * chans), BF16),
            vm((rows, chans), BF16),
            vm((rows // 2, 2 * chans), BF16),
            vm((2, rows // 2, 2 * chans), BF16),
            vm((rows, chans), F32),
            vm((3, rows + 2 * width, chans), BF16),
            vm((rows, chans), F32),
            vm((rows, chans), F32),
            vm((3, depth, chans), F32),
            vm((2, 2, depth, n_tm * lanes), F32),
            vm((2, depth, n_tm * lanes), F32),
            vm((2, depth, n_tm // 2 * lanes), BF16),
            vm((2, depth, n_tm // 2 * lanes), BF16),
            vm((n_tm, depth, lanes), F32),
            vm((n_tm, depth, lanes), BF16),
            vm((n_tm, depth, lanes), BF16),
            vm((n_tm, depth, lanes), BF16),
            dma((4,)),
            dma((3,)),
            dma((13,)),
            dma((13,)),
            dma((16,)),
            dma((16,)),
            dma((4,)),
            dma((4,)),
            dma((2 * n_tm,)),
            dma((2 * n_tm,)),
        ],
        compiler_params=pltpu.CompilerParams(
            collective_id=0, has_side_effects=True, vmem_limit_bytes=62 * 2**20
        ),
        name="block",
    )(
        video.reshape(rows, chans), spatial_w, spatial_b, temporal_w,
        cotangent.reshape(rows, chans),
    )
    shapes = tuple(jax.ShapeDtypeStruct(array.shape, F32) for array in results)
    out, gv, gt = pl.pallas_call(
        hand_over,
        out_shape=shapes,
        in_specs=[any_spec] * 3,
        out_specs=(any_spec,) * 3,
        scratch_shapes=[vm(shape.shape, F32) for shape in shapes] + [dma((12,)), dma((12,))],
        compiler_params=pltpu.CompilerParams(vmem_limit_bytes=62 * 2**20),
        name="hand_over",
    )(*results)
    return out.reshape(video.shape), gv.reshape(video.shape), gt


def padded_2(cells, sides, width):
    for axis, dim in sides:
        count = lax.axis_size(axis)
        ends = count - 1
        head = lax.slice_in_dim(cells, 0, width, axis=dim)
        tail = lax.slice_in_dim(cells, cells.shape[dim] - width, cells.shape[dim], axis=dim)
        cells = jnp.concatenate(
            [
                lax.ppermute(tail, axis, [(i, (i + 1) % count) for i in range(ends)]),
                cells,
                lax.ppermute(head, axis, [((i + 1) % count, i) for i in range(ends)]),
            ],
            axis=dim,
        )
    return cells


def native(video, spatial_w, spatial_b, temporal_w, cotangent):
    clips, frames, height, width, chans = video.shape
    row_count = clips * frames * height * width
    pads = ((0, 0), (0, 0), (1, 1), (1, 1), (0, 0))
    padded = jnp.pad(video.astype(BF16), pads)
    temporal_b = temporal_w.astype(BF16)
    spatial_all = lax.all_gather(spatial_w, "clip", axis=1, tiled=True)
    temporal_all = lax.all_gather(temporal_b, "clip", axis=1, tiled=True)
    spatial = jnp.zeros((row_count, chans), F32)
    for y in range(3):
        for x in range(3):
            window = padded[:, :, y : y + height, x : x + width, :].reshape(row_count, chans)
            spatial = spatial + nn_dot(window, spatial_all[3 * y + x])
    spatial = spatial + spatial_b
    sigmoid_s = jax.nn.sigmoid(spatial)
    hidden = (spatial * sigmoid_s).astype(BF16).reshape(video.shape)
    hidden_pad = padded_2(hidden, (("tm", 1),), 1)
    cot_b = cotangent.astype(BF16)
    cot_flat = cot_b.reshape(row_count, chans)
    cot_pad = padded_2(cot_b, (("tm", 1),), 1)
    temporal = jnp.zeros((row_count, chans), F32)
    grad_hidden = jnp.zeros((row_count, chans), F32)
    grads = []
    for k in range(3):
        shifted_hid = hidden_pad[:, k : k + frames].reshape(row_count, chans)
        temporal = temporal + nn_dot(shifted_hid, temporal_all[k])
        shifted_cot = cot_pad[:, 2 - k : 2 - k + frames].reshape(row_count, chans)
        grad_hidden = grad_hidden + transpose_dot(shifted_cot, temporal_all[k])
        grads.append(outer_dot(shifted_hid, cot_flat))
    total_rows = row_count * lax.axis_size("tm") * lax.axis_size("clip")
    summed = lax.psum(jnp.stack(grads), "tm")
    owned = lax.psum_scatter(summed, "clip", scatter_dimension=1, tiled=True)
    grad_spatial = (grad_hidden * sigmoid_s * (1.0 + spatial * (1.0 - sigmoid_s))).astype(BF16)
    grad_frames = jnp.pad(grad_spatial.reshape(video.shape), pads)
    grad_acc = cotangent.reshape(row_count, chans)
    for y in range(3):
        for x in range(3):
            window = grad_frames[:, :, 2 - y : 2 - y + height, 2 - x : 2 - x + width, :]
            window = window.reshape(row_count, chans)
            grad_acc = grad_acc + transpose_dot(window, spatial_all[3 * y + x])
    return (
        video + temporal.reshape(video.shape),
        grad_acc.reshape(video.shape),
        owned * (1.0 / math.sqrt(total_rows)),
    )


def solution(mesh):
    n_tm, n_clip = mesh.shape["tm"], mesh.shape["clip"]

    def on_device(video, spatial_w, spatial_b, temporal_w, cotangent):
        args = (video, spatial_w, spatial_b, temporal_w, cotangent)
        one_frame = video.shape[0] == 1 and video.shape[1] == 1
        if one_frame and spatial_w.shape[1] % 16 == 0 and n_clip == 4 and n_tm % 4 == 0:
            return fused(n_tm, n_clip, *args)
        return native(*args)

    return jax.shard_map(
        on_device,
        mesh=mesh,
        in_specs=(
            P("clip", "tm", None, None, None),
            P(None, "clip", None),
            P(),
            P(None, "clip", None),
            P("clip", "tm", None, None, None),
        ),
        out_specs=(
            P("clip", "tm", None, None, None),
            P("clip", "tm", None, None, None),
            P(None, "clip", None),
        ),
        check_vma=False,
    )
```
